512 devices in a mesh: dp: 16 (over z), feat: 32 (over y, x, core).
Axes of the slice: x: 4, y: 4, z: 16, core: 2. Of those that a mesh axis runs over, the one named last changes fastest.
Arguments:
- earlier: bfloat16 [3, 16384, 10240], P(None, 'feat', 'dp'), may hold values from -6 to 6
- mix_weights: float32 [3], replicated, may hold values from 0.3 to 1
- destinations: int32 [10240], replicated, may hold values from -1 to 8191, as said below
- cotangent: bfloat16 [16384, 8192], P('feat', 'dp'), may hold values from -6 to 6
- right_gate: bfloat16 [128, 128, 128], P('feat'), may hold values from -0.5 to 0.5
- left_gate: bfloat16 [128, 128, 128], P('feat'), may hold values from -0.5 to 0.5
- right_up: bfloat16 [128, 128, 128], P('feat'), may hold values from -0.5 to 0.5
- left_up: bfloat16 [128, 128, 128], P('feat'), may hold values from -0.5 to 0.5
- right_down: bfloat16 [128, 128, 128], P('feat'), may hold values from -0.5 to 0.5
- left_down: bfloat16 [128, 128, 128], P('feat'), may hold values from -0.5 to 0.5
Outputs:
- output: bfloat16 [16384, 8192], P('feat', 'dp')
- mixed_grad: bfloat16 [16384, 10240], P('feat', 'dp')
- grad_right_gate: float32 [128, 128, 128], P('feat', 'dp')
- grad_left_gate: float32 [128, 128, 128], P('feat', 'dp')
- grad_right_up: float32 [128, 128, 128], P('feat', 'dp')
- grad_left_up: float32 [128, 128, 128], P('feat', 'dp')
- grad_right_down: float32 [128, 128, 128], P('feat', 'dp')
- grad_left_down: float32 [128, 128, 128], P('feat', 'dp')
The draws below stay inside these ranges and needn't reach their ends.
Inputs may be any that keep to these rules, and one draw needn't show every extreme that they name: `destinations`: every packed row 0 to 8191 is named by exactly one slot; other slots hold -1. Among the 640 slots of one index of dp, at most 40 name rows of any one index of dp (packed rows of index g are g * 512 to (g + 1) * 512 - 1). In every draw one index of dp fills all its 640 slots, sending exactly 40 rows to every index.
All inputs are finite; a program needn't handle non-finite values.
Results may differ from the reference program's by a relative error of at most 0.0092.
Values may be sent and summed in bfloat16 or wider, within the bound.
A program may use at most 64 MiB of HBM per device.

```python
import jax
import jax.numpy as jnp
from jax import lax

B = 128
D = 16384
DEPTH = 3
TOK_DEV = 512
TOKENS = 8192
ROWS_ALL = 10240
N_DP = 16


def draw_destinations(key, part):
    groups = N_DP
    tok_rows = TOK_DEV
    cap_rows = 5 * TOK_DEV // (4 * N_DP)
    slot_count = 5 * TOK_DEV // 4
    others = groups - 1
    key_list = jax.random.split(key, 5)
    full_source = jax.random.randint(key_list[0], (), 0, groups)
    remainder = tok_rows - cap_rows
    base_count = remainder // others
    extra_count = remainder % others
    reach_limit = min(base_count - 1, cap_rows - base_count - 1)
    position = jnp.arange(others)
    drawn_counts = base_count + (position < extra_count).astype(jnp.int32)
    pair_count = others // 2
    moves = jax.random.randint(key_list[1], (groups, pair_count), 0, reach_limit + 1)
    pair_index = jnp.minimum(position // 2, pair_count - 1)
    signs = jnp.where(position % 2 == 0, 1, -1)
    paired = position // 2 < pair_count
    counts = drawn_counts[None, :] + jnp.where(paired[None, :], signs[None, :] * moves[:, pair_index], 0)
    shuffles = jax.vmap(lambda sub: jax.random.permutation(sub, others))(jax.random.split(key_list[2], groups))
    sources = (full_source + 1 + shuffles) % groups
    columns = jnp.broadcast_to(jnp.arange(groups)[:, None], (groups, others))
    matrix = jnp.zeros((groups, groups), jnp.int32).at[sources, columns].set(counts.astype(jnp.int32))
    matrix = matrix.at[full_source, :].set(cap_rows)
    live_rows = jnp.sum(matrix, axis=1)
    upper = jnp.cumsum(matrix, axis=1)
    lower = upper - matrix
    earlier_in = jnp.cumsum(matrix, axis=0) - matrix
    scores = jax.random.randint(key_list[3], (groups, slot_count), 0, 1 << 20) * slot_count + jnp.arange(slot_count)[None, :]
    ranks = jnp.argsort(jnp.argsort(scores, axis=1, stable=True), axis=1, stable=True).astype(jnp.int32)
    slot_orders = jax.vmap(lambda sub: jax.random.permutation(sub, tok_rows))(jax.random.split(key_list[4], groups)).astype(jnp.int32)

    def one_source(row_ranks, row_upper, row_lower, row_before, live_count):
        target = jnp.minimum(jnp.sum((row_ranks[:, None] >= row_upper[None, :]).astype(jnp.int32), axis=1), groups - 1)
        local_index = row_ranks - row_lower[target]
        ahead = jnp.clip(row_before[target] + local_index, 0, tok_rows - 1)
        chosen = slot_orders[target, ahead]
        return jnp.where(row_ranks < live_count, target * tok_rows + chosen, -1)
    table = jax.vmap(one_source)(ranks, upper, lower, earlier_in, live_rows)
    return table.reshape(-1).astype(jnp.int32)


def block_scale(rng, dims, cuts, low, high):
    def one(axis_at, shards_of):
        steps = jax.random.uniform(jax.random.fold_in(jax.random.fold_in(rng, 6), axis_at), (shards_of,), jnp.float32, low / len(cuts), high / len(cuts))
        return jnp.repeat(jnp.exp(steps), dims[axis_at] // shards_of).reshape((-1,) + (1,) * (len(dims) - axis_at - 1))

    loudness = one(*cuts[0])
    for cut in cuts[1:]:
        loudness = loudness * one(*cut)
    return loudness


def centred(key, dims, deviation, most, pieces=(), kind=jnp.bfloat16):
    entries = deviation * jax.random.normal(key, dims, jnp.float32)
    if pieces:
        entries = entries * block_scale(key, dims, pieces, -0.22, 0.18)
    return jnp.clip(entries, -most, most).astype(kind)


def setup_inputs(seed: int = 0) -> dict:
    key_of = jax.random.split(jax.random.key(seed), 11)
    return {
        "earlier": centred(key_of[0], (DEPTH, D, ROWS_ALL), 1.0, 6.0, ((1, 32), (2, 16))),
        "mix_weights": jnp.clip(jax.random.uniform(key_of[1], (DEPTH,), jnp.float32, 0.3, 1.0), 0.3, 1.0),
        "destinations": draw_destinations(jax.random.fold_in(key_of[10], 71), 0),
        "cotangent": centred(key_of[3], (D, TOKENS), 1.0, 6.0, ((0, 32), (1, 16))),
        "right_gate": centred(key_of[4], (B, B, B), B ** -0.5, 0.5, ((0, 32),)),
        "left_gate": centred(key_of[5], (B, B, B), B ** -0.5, 0.5, ((0, 32),)),
        "right_up": centred(key_of[6], (B, B, B), B ** -0.5, 0.5, ((0, 32),)),
        "left_up": centred(key_of[7], (B, B, B), B ** -0.5, 0.5, ((0, 32),)),
        "right_down": centred(key_of[8], (B, B, B), B ** -0.5, 0.5, ((0, 32),)),
        "left_down": centred(key_of[9], (B, B, B), B ** -0.5, 0.5, ((0, 32),)),
    }


def right_apply(values, right_factor):
    return jnp.einsum('ijt,ijo->iot', values.astype(jnp.float32), right_factor.astype(jnp.float32)).astype(jnp.bfloat16)

def left_apply(spread, left_factor):
    return jnp.einsum('iot,oip->pot', spread.astype(jnp.float32), left_factor.astype(jnp.float32)).astype(jnp.bfloat16)

def left_back(out_grad, left_factor):
    return jnp.einsum('pot,oip->iot', out_grad.astype(jnp.float32), left_factor.astype(jnp.float32)).astype(jnp.bfloat16)

def right_back(spread_grad, right_factor):
    return jnp.einsum('iot,ijo->ijt', spread_grad.astype(jnp.float32), right_factor.astype(jnp.float32))

def left_grad(spread, out_grad):
    return jnp.einsum('iot,pot->oip', spread.astype(jnp.float32), out_grad.astype(jnp.float32))

def right_grad(values, spread_grad):
    return jnp.einsum('ijt,iot->ijo', values.astype(jnp.float32), spread_grad.astype(jnp.float32))

def gelu_slope(values):
    return jax.vjp(jax.nn.gelu, values)[1](jnp.ones_like(values))[0]

def mixer_block(inputs, out_grads, factors):
    right_gate, left_gate, right_up, left_up, right_down, left_down = factors
    gate_spread = right_apply(inputs, right_gate)
    up_spread = right_apply(inputs, right_up)
    gate_out = left_apply(gate_spread, left_gate)
    up_out = left_apply(up_spread, left_up)
    gate_f = gate_out.astype(jnp.float32)
    up_f = up_out.astype(jnp.float32)
    hidden = (jax.nn.gelu(gate_f) * up_f).astype(jnp.bfloat16)
    down_spread = right_apply(hidden, right_down)
    output = left_apply(down_spread, left_down)
    down_spread_grad = left_back(out_grads, left_down)
    grad_left_down = left_grad(down_spread, out_grads)
    hidden_grad = right_back(down_spread_grad, right_down)
    grad_right_down = right_grad(hidden, down_spread_grad)
    gate_grad = (hidden_grad * up_f * gelu_slope(gate_f)).astype(jnp.bfloat16)
    up_grad = (hidden_grad * jax.nn.gelu(gate_f)).astype(jnp.bfloat16)
    gate_spread_grad = left_back(gate_grad, left_gate)
    up_spread_grad = left_back(up_grad, left_up)
    grad_left_gate = left_grad(gate_spread, gate_grad)
    grad_left_up = left_grad(up_spread, up_grad)
    input_grad = (right_back(gate_spread_grad, right_gate) + right_back(up_spread_grad, right_up)).astype(jnp.bfloat16)
    grad_right_gate = right_grad(inputs, gate_spread_grad)
    grad_right_up = right_grad(inputs, up_spread_grad)
    grads = (grad_right_gate, grad_left_gate, grad_right_up, grad_left_up, grad_right_down, grad_left_down)
    return (output, input_grad, grads)

def reference(earlier, mix_weights, destinations, cotangent, right_gate, left_gate, right_up, left_up, right_down, left_down):
    factors = (right_gate, left_gate, right_up, left_up, right_down, left_down)
    live = destinations >= 0
    source_of = jnp.zeros((TOKENS,), jnp.int32).at[jnp.where(live, destinations, TOKENS).astype(jnp.int32)].set(jnp.arange(ROWS_ALL, dtype=jnp.int32), mode='drop')

    def step(sums_carry, group):
        start = (group * TOK_DEV).astype(jnp.int32)
        picks = lax.dynamic_slice_in_dim(source_of, start, TOK_DEV)
        columns = jnp.take(earlier, picks, axis=2).astype(jnp.float32)
        averaged = jnp.zeros((D, TOK_DEV), jnp.float32)
        for depth_index in range(DEPTH):
            averaged = averaged + mix_weights[depth_index] * columns[depth_index]
        inputs = averaged.astype(jnp.bfloat16).reshape(B, B, TOK_DEV)
        out_grads = lax.dynamic_slice_in_dim(cotangent, start, TOK_DEV, 1).reshape(B, B, TOK_DEV)
        output, input_grad, grads = mixer_block(inputs, out_grads, factors)
        new_sums = tuple((total + piece for total, piece in zip(sums_carry, grads)))
        return (new_sums, (output.reshape(D, TOK_DEV), input_grad.reshape(D, TOK_DEV)))
    zero_sums = tuple((jnp.zeros((B, B, B), jnp.float32) for factor in factors))
    sums_final, (outputs, input_grads) = lax.scan(step, zero_sums, jnp.arange(N_DP, dtype=jnp.int32))
    output = jnp.moveaxis(outputs, 0, 1).reshape(D, TOKENS)
    packed_grad = jnp.moveaxis(input_grads, 0, 1).reshape(D, TOKENS)
    picked = jnp.take(packed_grad, jnp.where(live, destinations, 0).astype(jnp.int32), axis=1)
    mixed_grad = jnp.where(live[None, :], picked, jnp.zeros((), jnp.bfloat16))
    grad_scale = TOKENS ** (-0.5)
    scaled = tuple((total * grad_scale for total in sums_final))
    return (output, mixed_grad, scaled[0], scaled[1], scaled[2], scaled[3], scaled[4], scaled[5])
```

```python
import jax
import jax.numpy as jnp
from jax import lax
from jax.experimental import pallas as pl
from jax.experimental.pallas import tpu as pltpu
from jax.sharding import PartitionSpec as P

MESH = pl.DeviceIdType.MESH
BF = jnp.bfloat16
F32 = jnp.float32
I32 = jnp.int32

GATE1, UP1, GATE2, UP2, DOWN1, DOWN2, CT, DSG, GGRAD, UGRAD, GSG, USG = range(12)
WG, WGT, WU, WUT, WD, WDT, LG, LGT, LU, LUT, LD, LDT = range(12)


def dot_nn(a, b):
    return lax.dot_general(a, b, (((1,), (0,)), ((), ())), preferred_element_type=F32)


def dot_nt(a, b):
    return lax.dot_general(a, b, (((1,), (1,)), ((), ())), preferred_element_type=F32)


def dot_tn(a, b):
    return lax.dot_general(a, b, (((0,), (0,)), ((), ())), preferred_element_type=F32)


def tiles(total, width):
    return [(s, min(width, total - s)) for s in range(0, total, width)]


def loop(count, step):
    def run(i, carry):
        step(i)
        return carry

    lax.fori_loop(0, count, run, 0)


def at(i, width):
    return pl.ds(pl.multiple_of(i * width, width), width)


def iota(shape, dim):
    return lax.broadcasted_iota(I32, shape, dim)


def kernel(
    weights_ref, earlier_ref, dest_ref, cot_ref, rg_ref, lg_ref, ru_ref, lu_ref, rd_ref, ld_ref,
    out_ref, mgrad_ref, g0_ref, g1_ref, g2_ref, g3_ref, g4_ref, g5_ref,
    send, recv, zsend, zrecv, gsend, grecv, mats, perm1t, perm1, perm2t, perm2, tmp_a, tmp_b,
    mixed, hidden, act, slope, pick_rows, pick_slots, pick_wide, prefix, ranks, row_of, cperm,
    ssem, rsem, zssem, zrsem,
):
    n_feat, slab, slots = send.shape[1:]
    n_dp, lanes_out, width = zsend.shape[1:]
    feats, rows = cot_ref.shape
    me_f = lax.axis_index("feat")
    me_g = lax.axis_index("dp")
    cap = lanes_out // 4
    n_lanes = n_dp * cap
    main = n_dp * 32

    def feat_peer(k):
        return lax.rem(me_f + lax.rem(k * 11, n_feat), n_feat)

    def dp_peer(i):
        return lax.rem(me_g + 8 + ((i + 1) // 2) * (1 - 2 * lax.rem(i, 2)), n_dp)

    barrier = pltpu.get_barrier_semaphore()
    loop(n_feat - 1, lambda i: pl.semaphore_signal(
        barrier, inc=1, device_id={"feat": feat_peer(i + 1)}, device_id_type=MESH))
    loop(n_dp - 1, lambda i: pl.semaphore_signal(
        barrier, inc=1, device_id={"dp": dp_peer(i)}, device_id_type=MESH))

    def start_feat(n):
        def step(i):
            peer = feat_peer(i + 1)
            pltpu.make_async_remote_copy(
                src_ref=send.at[n, peer], dst_ref=recv.at[n, me_f],
                send_sem=ssem.at[n], recv_sem=rsem.at[n],
                device_id={"feat": peer}, device_id_type=MESH,
            ).start()

        loop(n_feat - 1, step)
        recv[n, me_f] = send[n, me_f]

    def feat_all(n):
        return pltpu.make_async_remote_copy(
            src_ref=send.at[n, pl.ds(0, n_feat - 1)], dst_ref=recv.at[n, pl.ds(0, n_feat - 1)],
            send_sem=ssem.at[n], recv_sem=rsem.at[n],
            device_id={"feat": feat_peer(1)}, device_id_type=MESH,
        )

    def dp_bufs(n):
        return (zsend.at[n], zrecv.at[n]) if n < 2 else (gsend.at[n - 2], grecv.at[n - 2])

    def start_dp(n):
        source, target = dp_bufs(n)

        def step(i):
            peer = dp_peer(i)
            pltpu.make_async_remote_copy(
                src_ref=source.at[peer], dst_ref=target.at[me_g],
                send_sem=zssem.at[n], recv_sem=zrsem.at[n],
                device_id={"dp": peer}, device_id_type=MESH,
            ).start()

        loop(n_dp - 1, step)
        target[me_g] = source[me_g]

    def dp_all(n):
        source, target = dp_bufs(n)
        return pltpu.make_async_remote_copy(
            src_ref=source.at[pl.ds(0, n_dp - 1)], dst_ref=target.at[pl.ds(0, n_dp - 1)],
            send_sem=zssem.at[n], recv_sem=zrsem.at[n],
            device_id={"dp": dp_peer(0)}, device_id_type=MESH,
        )

    def build_perms():
        def step(i):
            here = at(i, 128)
            r, c = iota((128, feats), 0) + i * 128, iota((128, feats), 1)
            q, a, b = r >> 4, (r >> 2) & 3, r & 3
            perm1t[here, :] = (c == a * 128 + 4 * q + b).astype(F32).astype(BF)
            perm2t[here, :] = (c == b * 128 + 4 * q + a).astype(F32).astype(BF)
            q, a, b = c >> 4, (c >> 2) & 3, c & 3
            perm1[here, :] = (r == a * 128 + 4 * q + b).astype(F32).astype(BF)
            perm2[here, :] = (r == b * 128 + 4 * q + a).astype(F32).astype(BF)

        loop(feats // 128, step)

    def square(dst, first, second, dot):
        def step(i):
            dst[at(i, 128), :] = dot(first[at(i, 128), :], second[...]).astype(BF)

        loop(feats // 128, step)

    def build_right(factor, w, wt):
        def step(i):
            w[:, at(i, 128)] = dot_nt(perm1t[:, at(i, 128)], factor[i]).astype(BF)
            wt[at(i, 128), :] = dot_nt(factor[i], perm1t[:, at(i, 128)]).astype(BF)

        loop(4, step)

    def build_left(factor, w, wt):
        def step(i):
            tmp_a[:, at(i, 128)] = dot_nn(perm2t[:, at(i, 128)], factor[i]).astype(BF)
            tmp_b[:, at(i, 128)] = dot_nt(perm2t[:, at(i, 128)], factor[i]).astype(BF)

        loop(4, step)
        square(wt, tmp_a.at[:, pl.ds(0, feats)], perm2t, dot_nt)
        square(w, tmp_b.at[:, pl.ds(0, feats)], perm2t, dot_nt)

    def flat(ref, n, s, w):
        return ref[n, :, :, pl.ds(s, w)].reshape(feats, w)

    def got(n):
        return lambda s, w: flat(recv, n, s, w)

    def plain(ref):
        return lambda s, w: ref[:, pl.ds(s, w)]

    def to_send(n):
        def put(s, w, value):
            send[n, :, :, pl.ds(s, w)] = value.astype(BF).reshape(n_feat, slab, w)

        return put

    def to_ref(ref):
        def put(s, w, value):
            ref[:, pl.ds(s, w)] = value.astype(ref.dtype)

        return put

    def product(put, mat, load, total=slots, step=256):
        for s, w in tiles(total, step):
            put(s, w, dot_nn(mat[...], load(s, w)))

    def to_lanes(n, pick, load):
        rest = []
        for c in range(4):
            value = dot_nt(pick[...], load(c))
            zsend[n, :, pl.ds(c * 32, 32), :] = value[:main].reshape(n_dp, 32, width).astype(BF)
            rest.append(value[main:].reshape(n_dp, 8, width))
        for h in range(2):
            pair = jnp.concatenate(rest[2 * h : 2 * h + 2], axis=1).astype(BF)
            zsend[n, :, pl.ds(128 + 16 * h, 16), :] = pair

    def from_lanes(n, pick, c):
        head = zrecv[n, :, pl.ds(c * 32, 32), :].reshape(main, width)
        pair = zrecv[n, :, pl.ds(128 + 16 * (c // 2), 16), :].astype(F32)
        tail = pair[:, 8 * (c % 2) : 8 * (c % 2) + 8, :].reshape(n_dp * 8, width).astype(BF)
        return dot_tn(jnp.concatenate([head, tail], axis=0), pick[...])

    def grad(n, first, second):
        parts = []
        for c in range(4):
            here = pl.ds(c * 128, 128)
            parts.append(dot_nt(first[here, :], second[here, :]).reshape(n_dp, 8, 128))
        gsend[n - 2] = jnp.concatenate(parts, axis=1).astype(BF)
        start_dp(n)

    def grad_left(n, spread, outgrad):
        product(to_ref(tmp_a), perm2, got(spread))
        product(to_ref(tmp_b), perm2, got(outgrad))
        grad(n, tmp_a, tmp_b)

    def finish_grad(n, ref):
        dp_all(n).wait_recv()
        total = jnp.sum(grecv[n - 2].astype(F32), axis=0) * ((rows * n_dp) ** (-0.5))
        ref[...] = total.reshape(4, 8, 128)

    def mix(i):
        here = at(i, 64)
        total = jnp.zeros((64, slots), F32)
        for k in range(earlier_ref.shape[0]):
            total = total + weights_ref[k] * earlier_ref[k, here, :].astype(F32)
        mixed[here, :] = total.astype(BF)

    loop(feats // 64, mix)
    build_perms()
    build_right(rg_ref, mats.at[WG], mats.at[WGT])
    build_right(ru_ref, mats.at[WU], mats.at[WUT])
    product(to_send(GATE1), mats.at[WG], plain(mixed))
    product(to_send(UP1), mats.at[WU], plain(mixed))

    def prefix_step(i):
        r, c = iota((128, slots), 0) + i * 128, iota((128, slots), 1)
        prefix[at(i, 128), :] = (r < c).astype(F32).astype(BF)

    loop(slots // 128, prefix_step)
    dest = dest_ref[...]
    inside = (dest >> 9) == me_g
    rank = dot_nn(inside.astype(F32).astype(BF), prefix[...])
    ranks[...] = jnp.where(inside, rank, -1.0)
    row_of[...] = (dest - me_g * rows).astype(F32)

    def rows_step(s):
        hit = iota((cap, slots), 0).astype(F32) == ranks[pl.ds(s, 1), :]
        row = jnp.sum(jnp.where(hit, row_of[pl.ds(s, 1), :] + 1.0, 0.0), axis=1, keepdims=True)
        chosen = (row == (iota((cap, rows), 1) + 1).astype(F32)).astype(F32)
        pick_wide[at(s, 32), :] = chosen[:32]
        pick_wide[pl.ds(pl.multiple_of(main + s * 8, 8), 8), :] = chosen[32:]

    loop(n_dp, rows_step)

    def narrow_step(i):
        pick_rows[at(i, 128), :] = pick_wide[at(i, 128), :].astype(BF)

    loop(n_lanes // 128, narrow_step)
    mine = dest_ref[pl.ds(me_g, 1), :]
    target = mine >> 9
    member = iota((n_dp, slots), 0) == target
    rank = dot_nn(member.astype(F32).astype(BF), prefix[...])
    rank = jnp.sum(jnp.where(member, rank, 0.0), axis=0, keepdims=True).astype(I32)
    lane = jnp.where(rank < 32, target * 32 + rank, main + target * 8 + rank - 32)
    lane = jnp.where(mine >= 0, lane, -1)

    def slots_step(i):
        pick_slots[at(i, 128), :] = (iota((128, slots), 0) + i * 128 == lane).astype(F32).astype(BF)

    loop(n_lanes // 128, slots_step)
    product(to_ref(cperm), perm1t, plain(cot_ref), total=rows)
    to_lanes(0, pick_rows, lambda c: cperm[pl.ds(c * 128, 128), :])

    pl.semaphore_wait(barrier, n_feat + n_dp - 2)
    start_feat(GATE1)
    start_dp(0)
    start_feat(UP1)

    build_left(lg_ref, mats.at[LG], mats.at[LGT])
    build_left(lu_ref, mats.at[LU], mats.at[LUT])
    build_left(ld_ref, mats.at[LD], mats.at[LDT])
    build_right(rd_ref, tmp_a.at[:, pl.ds(0, feats)], tmp_b.at[:, pl.ds(0, feats)])
    square(mats.at[WD], tmp_a.at[:, pl.ds(0, feats)], perm1t, dot_nt)
    square(mats.at[WDT], perm1t, tmp_b.at[:, pl.ds(0, feats)], dot_nn)

    feat_all(GATE1).wait_recv()
    product(to_send(GATE2), mats.at[LG], got(GATE1))
    start_feat(GATE2)
    feat_all(UP1).wait_recv()
    product(to_send(UP2), mats.at[LU], got(UP1))
    start_feat(UP2)

    dp_all(0).wait_recv()
    for c in range(4):
        value = from_lanes(0, pick_slots, c).astype(BF)
        send[CT, pl.ds(c * 8, 8)] = value.reshape(8, slab, slots)
    start_feat(CT)

    feat_all(GATE2).wait_recv()
    feat_all(UP2).wait_recv()

    def activate(i):
        here = at(i, 128)
        gate = recv[GATE2, :, :, here].reshape(feats, 128).astype(F32)
        up = recv[UP2, :, :, here].reshape(feats, 128).astype(F32)
        scale = 0.7978845608028654
        square_ = gate * gate
        t = jnp.tanh(scale * (gate + 0.044715 * (square_ * gate)))
        half = 0.5 * (1.0 + t)
        gelu = gate * half
        act[:, here] = gelu
        inner = scale * (1.0 + 3 * 0.044715 * square_)
        slope[:, here] = up * (half + 0.5 * gate * ((1.0 - t * t) * inner))
        hidden[:, here] = (gelu * up).astype(BF)

    loop(slots // 128, activate)
    product(to_send(DOWN1), mats.at[WD], plain(hidden))
    start_feat(DOWN1)

    feat_all(CT).wait_recv()
    product(to_send(DSG), mats.at[LDT], got(CT))
    start_feat(DSG)

    feat_all(DOWN1).wait_recv()
    product(to_send(DOWN2), mats.at[LD], got(DOWN1))
    start_feat(DOWN2)

    feat_all(DSG).wait_recv()
    for s, w in tiles(slots, 128):
        hidden_grad = dot_nn(mats[WDT], flat(recv, DSG, s, w))
        to_send(GGRAD)(s, w, hidden_grad * slope[:, pl.ds(s, w)])
        to_send(UGRAD)(s, w, hidden_grad * act[:, pl.ds(s, w)])
    start_feat(GGRAD)
    start_feat(UGRAD)

    grad_left(7, DOWN1, CT)
    product(to_ref(tmp_a), perm1, plain(hidden))
    product(to_ref(tmp_b), perm1, got(DSG))
    grad(6, tmp_a, tmp_b)

    feat_all(GGRAD).wait_recv()
    product(to_send(GSG), mats.at[LGT], got(GGRAD))
    start_feat(GSG)
    feat_all(UGRAD).wait_recv()
    product(to_send(USG), mats.at[LUT], got(UGRAD))
    start_feat(USG)

    feat_all(DOWN2).wait_recv()
    to_lanes(1, pick_slots, lambda c: recv[DOWN2, pl.ds(c * 8, 8)].reshape(128, slots))
    start_dp(1)

    grad_left(3, GATE1, GGRAD)
    grad_left(5, UP1, UGRAD)

    feat_all(GSG).wait_recv()
    product(to_ref(tmp_b), perm1, got(GSG))
    grad(2, mixed, tmp_b)
    feat_all(USG).wait_recv()
    product(to_ref(tmp_b), perm1, got(USG))
    grad(4, mixed, tmp_b)
    for s, w in tiles(slots, 256):
        value = dot_nn(mats[WGT], flat(recv, GSG, s, w)) + dot_nn(mats[WUT], flat(recv, USG, s, w))
        mgrad_ref[:, pl.ds(s, w)] = value.astype(BF)

    dp_all(1).wait_recv()
    for c in range(4):
        cperm[pl.ds(c * 128, 128), :] = from_lanes(1, pick_rows, c).astype(BF)
    product(to_ref(out_ref), perm1, plain(cperm), total=rows)

    finish_grad(6, g4_ref)
    finish_grad(7, g5_ref)
    finish_grad(3, g1_ref)
    finish_grad(5, g3_ref)
    finish_grad(2, g0_ref)
    finish_grad(4, g2_ref)
    for n in range(12):
        feat_all(n).wait_send()
    for n in range(8):
        dp_all(n).wait_send()


def body(earlier, mix_weights, destinations, cotangent, *factors):
    n_feat, n_dp = lax.axis_size("feat"), lax.axis_size("dp")
    feats, slots = earlier.shape[1:]
    rows = cotangent.shape[1]
    slab = feats // n_feat
    cap = slots // n_dp
    grad_shape = (factors[0].shape[0], factors[0].shape[1] // n_dp, factors[0].shape[2])
    vmem = pl.BlockSpec(memory_space=pltpu.VMEM)
    wide = pltpu.VMEM((feats, slots), BF)
    square = pltpu.VMEM((feats, feats), BF)
    return pl.pallas_call(
        kernel,
        out_shape=(
            jax.ShapeDtypeStruct((feats, rows), BF),
            jax.ShapeDtypeStruct((feats, slots), BF),
        )
        + (jax.ShapeDtypeStruct(grad_shape, F32),) * 6,
        in_specs=[pl.BlockSpec(memory_space=pltpu.SMEM)] + [vmem] * 9,
        out_specs=(vmem,) * 8,
        scratch_shapes=[
            pltpu.VMEM((12, n_feat, slab, slots), BF),
            pltpu.VMEM((12, n_feat, slab, slots), BF),
            pltpu.VMEM((2, n_dp, 4 * cap, 128), BF),
            pltpu.VMEM((2, n_dp, 4 * cap, 128), BF),
            pltpu.VMEM((6, n_dp, 32, 128), BF),
            pltpu.VMEM((6, n_dp, 32, 128), BF),
            pltpu.VMEM((12, feats, feats), BF),
            square, square, square, square,
            wide, wide, wide, wide,
            pltpu.VMEM((feats, slots), F32),
            pltpu.VMEM((feats, slots), F32),
            pltpu.VMEM((n_dp * cap, rows), BF),
            pltpu.VMEM((n_dp * cap, slots), BF),
            pltpu.VMEM((n_dp * cap, rows), F32),
            pltpu.VMEM((slots, slots), BF),
            pltpu.VMEM((n_dp, slots), F32),
            pltpu.VMEM((n_dp, slots), F32),
            pltpu.VMEM((feats, rows), BF),
            pltpu.SemaphoreType.DMA((12,)),
            pltpu.SemaphoreType.DMA((12,)),
            pltpu.SemaphoreType.DMA((8,)),
            pltpu.SemaphoreType.DMA((8,)),
        ],
        compiler_params=pltpu.CompilerParams(
            collective_id=0, has_side_effects=True, vmem_limit_bytes=60 << 20
        ),
    )(mix_weights, earlier, destinations.reshape(n_dp, slots), cotangent, *factors)


def solution(mesh):
    factor, grad = P("feat", None, None), P("feat", "dp", None)
    return jax.shard_map(
        body,
        mesh=mesh,
        in_specs=(P(None, "feat", "dp"), P(), P(), P("feat", "dp")) + (factor,) * 6,
        out_specs=(P("feat", "dp"), P("feat", "dp")) + (grad,) * 6,
        check_vma=False,
    )
```

```python
import jax
import jax.numpy as jnp
from jax import lax
from jax.experimental import pallas as pl
from jax.experimental.pallas import tpu as pltpu
from jax.sharding import PartitionSpec as P

MESH = pl.DeviceIdType.MESH
BF = jnp.bfloat16
F32 = jnp.float32
I32 = jnp.int32

GATE1, UP1, GATE2, UP2, DOWN1, DOWN2, CT, DSG, GGRAD, UGRAD, GSG, USG = range(12)
WG, WGT, WU, WUT, WD, WDT, LG, LGT, LU, LUT, LD, LDT = range(12)


def dot_nn(a, b):
    return lax.dot_general(a, b, (((1,), (0,)), ((), ())), preferred_element_type=F32)


def dot_nt(a, b):
    return lax.dot_general(a, b, (((1,), (1,)), ((), ())), preferred_element_type=F32)


def dot_tn(a, b):
    return lax.dot_general(a, b, (((0,), (0,)), ((), ())), preferred_element_type=F32)


def tiles(total, width):
    return [(s, min(width, total - s)) for s in range(0, total, width)]


def loop(count, step):
    def run(i, carry):
        step(i)
        return carry

    lax.fori_loop(0, count, run, 0)


def at(i, width):
    return pl.ds(pl.multiple_of(i * width, width), width)


def iota(shape, dim):
    return lax.broadcasted_iota(I32, shape, dim)


def kernel(
    weights_ref, earlier_in, dest_in, cot_in, rg_in, lg_in, ru_in, lu_in, rd_in, ld_in,
    out_ref, mgrad_ref, grads_ref,
    earlier_ref, dest_ref, cot_ref, factors, isem,
    send, recv, zsend, zrecv, gsend, gnear, gsum, gfar, dest_all, mats, perm1t, perm1, perm2t, perm2, tmp_a, tmp_b,
    mixed, hidden, act, slope, pick_rows, pick_slots, pick_wide, prefix, ranks, row_of, cperm,
    ssem, rsem, zssem, zrsem, nssem, nrsem, fssem, frsem,
):
    n_feat, slab, slots = send.shape[1:]
    n_dp, lanes_out, width = zsend.shape[1:]
    feats, rows = cot_in.shape
    me_f = lax.axis_index("feat")
    me_g = lax.axis_index("dp")
    cap = lanes_out // 4
    n_lanes = n_dp * cap
    main = n_dp * 32

    def feat_peer(k):
        return lax.rem(me_f + lax.rem(k * 11, n_feat), n_feat)

    def dp_peer(i):
        return lax.rem(me_g + 8 + ((i + 1) // 2) * (1 - 2 * lax.rem(i, 2)), n_dp)

    rg_ref, lg_ref, ru_ref, lu_ref, rd_ref, ld_ref = (factors.at[n] for n in range(6))
    loads = [
        pltpu.make_async_copy(source, target, isem.at[n])
        for n, (source, target) in enumerate((
            (earlier_in, earlier_ref), (rg_in, rg_ref), (ru_in, ru_ref), (dest_in, dest_ref),
            (cot_in, cot_ref), (lg_in, lg_ref), (lu_in, lu_ref), (rd_in, rd_ref), (ld_in, ld_ref),
        ))
    ]
    for load in loads:
        load.start()
    barrier = pltpu.get_barrier_semaphore()
    loop(n_feat - 1, lambda i: pl.semaphore_signal(
        barrier, inc=1, device_id={"feat": feat_peer(i + 1)}, device_id_type=MESH))
    loop(n_dp - 1, lambda i: pl.semaphore_signal(
        barrier, inc=1, device_id={"dp": dp_peer(i)}, device_id_type=MESH))

    def start_feat(n):
        def step(i):
            peer = feat_peer(i + 1)
            pltpu.make_async_remote_copy(
                src_ref=send.at[n, peer], dst_ref=recv.at[n, me_f],
                send_sem=ssem.at[n], recv_sem=rsem.at[n],
                device_id={"feat": peer}, device_id_type=MESH,
            ).start()

        loop(n_feat - 1, step)
        recv[n, me_f] = send[n, me_f]

    def feat_all(n):
        return pltpu.make_async_remote_copy(
            src_ref=send.at[n, pl.ds(0, n_feat - 1)], dst_ref=recv.at[n, pl.ds(0, n_feat - 1)],
            send_sem=ssem.at[n], recv_sem=rsem.at[n],
            device_id={"feat": feat_peer(1)}, device_id_type=MESH,
        )

    def start_dp(n):
        def step(i):
            peer = dp_peer(i)
            pltpu.make_async_remote_copy(
                src_ref=zsend.at[n, peer], dst_ref=zrecv.at[n, me_g],
                send_sem=zssem.at[n], recv_sem=zrsem.at[n],
                device_id={"dp": peer}, device_id_type=MESH,
            ).start()

        loop(n_dp - 1, step)
        zrecv[n, me_g] = zsend[n, me_g]

    def dp_all(n):
        return pltpu.make_async_remote_copy(
            src_ref=zsend.at[n, pl.ds(0, n_dp - 1)], dst_ref=zrecv.at[n, pl.ds(0, n_dp - 1)],
            send_sem=zssem.at[n], recv_sem=zrsem.at[n],
            device_id={"dp": dp_peer(0)}, device_id_type=MESH,
        )

    def near(n, h):
        return pltpu.make_async_remote_copy(
            src_ref=gsend.at[n, pl.ds(12 * h, 5)], dst_ref=gnear.at[n, h],
            send_sem=nssem.at[n, h], recv_sem=nrsem.at[n, h],
            device_id={"dp": lax.rem(me_g + (1, n_dp - 1)[h], n_dp)}, device_id_type=MESH,
        )

    def far(n, j):
        return pltpu.make_async_remote_copy(
            src_ref=gsum.at[n, j], dst_ref=gfar.at[n, j],
            send_sem=fssem.at[n], recv_sem=frsem.at[n],
            device_id={"dp": lax.rem(me_g + 2 * n_dp - 2 - 3 * j, n_dp)}, device_id_type=MESH,
        )

    def far_all(n):
        return pltpu.make_async_remote_copy(
            src_ref=gsum.at[n], dst_ref=gfar.at[n], send_sem=fssem.at[n], recv_sem=frsem.at[n],
            device_id={"dp": lax.rem(me_g + 1, n_dp)}, device_id_type=MESH,
        )

    def relay(n):
        near(n, 0).wait_recv()
        near(n, 1).wait_recv()
        total = gsend[n, pl.ds(6, 5)].astype(F32) + gnear[n, 0].astype(F32) + gnear[n, 1].astype(F32)
        gsum[n] = total.astype(BF)
        for j in range(5):
            far(n, j).start()

    def build_perms():
        def step(i):
            here = at(i, 128)
            r, c = iota((128, feats), 0) + i * 128, iota((128, feats), 1)
            q, a, b = r >> 4, (r >> 2) & 3, r & 3
            perm1t[here, :] = (c == a * 128 + 4 * q + b).astype(F32).astype(BF)
            perm2t[here, :] = (c == b * 128 + 4 * q + a).astype(F32).astype(BF)
            q, a, b = c >> 4, (c >> 2) & 3, c & 3
            perm1[here, :] = (r == a * 128 + 4 * q + b).astype(F32).astype(BF)
            perm2[here, :] = (r == b * 128 + 4 * q + a).astype(F32).astype(BF)

        loop(feats // 128, step)

    def square(dst, first, second):
        for s, w in tiles(feats, 256):
            dst[:, pl.ds(s, w)] = dot_nn(first[...], second[:, pl.ds(s, w)]).astype(BF)

    def build_right(factor, w):
        def step(i):
            w[:, at(i, 128)] = dot_nt(perm1t[:, at(i, 128)], factor[i]).astype(BF)

        loop(4, step)

    def build_right_back(factor, wt):
        def step(i):
            wt[at(i, 128), :] = dot_nt(factor[i], perm1t[:, at(i, 128)]).astype(BF)

        loop(4, step)

    def build_left(factor, w):
        def step(i):
            tmp_b[:, at(i, 128)] = dot_nt(perm2t[:, at(i, 128)], factor[i]).astype(BF)

        loop(4, step)
        square(w, tmp_b.at[:, pl.ds(0, feats)], perm2)

    def build_left_back(factor, wt):
        def step(i):
            tmp_a[:, at(i, 128)] = dot_nn(perm2t[:, at(i, 128)], factor[i]).astype(BF)

        loop(4, step)
        square(wt, tmp_a.at[:, pl.ds(0, feats)], perm2)

    def flat(ref, n, s, w):
        return ref[n, :, :, pl.ds(s, w)].reshape(feats, w)

    def got(n):
        return lambda s, w: flat(recv, n, s, w)

    def plain(ref):
        return lambda s, w: ref[:, pl.ds(s, w)]

    def to_send(n):
        def put(s, w, value):
            send[n, :, :, pl.ds(s, w)] = value.astype(BF).reshape(n_feat, slab, w)

        return put

    def to_ref(ref):
        def put(s, w, value):
            ref[:, pl.ds(s, w)] = value.astype(ref.dtype)

        return put

    def product(put, mat, load, total=slots, step=256):
        for s, w in tiles(total, step):
            put(s, w, dot_nn(mat[...], load(s, w)))

    def to_lanes(n, pick, load):
        rest = []
        for c in range(4):
            value = dot_nt(pick[...], load(c))
            zsend[n, :, pl.ds(c * 32, 32), :] = value[:main].reshape(n_dp, 32, width).astype(BF)
            rest.append(value[main:].reshape(n_dp, 8, width))
        for h in range(2):
            pair = jnp.concatenate(rest[2 * h : 2 * h + 2], axis=1).astype(BF)
            zsend[n, :, pl.ds(128 + 16 * h, 16), :] = pair

    def from_lanes(n, pick, c):
        head = zrecv[n, :, pl.ds(c * 32, 32), :].reshape(main, width)
        pair = zrecv[n, :, pl.ds(128 + 16 * (c // 2), 16), :].astype(F32)
        tail = pair[:, 8 * (c % 2) : 8 * (c % 2) + 8, :].reshape(n_dp * 8, width).astype(BF)
        return dot_tn(jnp.concatenate([head, tail], axis=0), pick[...])

    def grad(n, first, second):
        parts = []
        for c in range(4):
            here = pl.ds(c * 128, 128)
            parts.append(dot_nt(first[here, :], second[here, :]).reshape(n_dp, 8, 128))
        packed = jnp.concatenate(parts, axis=1).astype(BF)
        for g in range(n_dp):
            m = lax.rem(me_g + 2 * n_dp - 1 - g, n_dp)
            gsend[n, lax.rem(m, 3) * 6 + m // 3] = packed[g]
        near(n, 0).start()
        near(n, 1).start()

    def grad_left(n, spread, outgrad):
        product(to_ref(tmp_a), perm2, got(spread))
        product(to_ref(tmp_b), perm2, got(outgrad))
        grad(n, tmp_a, tmp_b)

    def finish_grad(n):
        far_all(n).wait_recv()
        total = gsend[n, 5].astype(F32) + jnp.sum(gfar[n].astype(F32), axis=0)
        grads_ref[n] = total * ((rows * n_dp) ** (-0.5))

    def mix(i):
        here = at(i, 64)
        total = jnp.zeros((64, slots), F32)
        for k in range(earlier_ref.shape[0]):
            total = total + weights_ref[k] * earlier_ref[k, here, :].astype(F32)
        mixed[here, :] = total.astype(BF)

    build_perms()
    loads[0].wait()
    loop(feats // 64, mix)
    loads[1].wait()
    build_right(rg_ref, mats.at[WG])
    product(to_send(GATE1), mats.at[WG], plain(mixed))
    loads[2].wait()
    build_right(ru_ref, mats.at[WU])
    product(to_send(UP1), mats.at[WU], plain(mixed))

    def prefix_step(i):
        r, c = iota((128, slots), 0) + i * 128, iota((128, slots), 1)
        prefix[at(i, 128), :] = (r < c).astype(F32).astype(BF)

    loop(slots // 128, prefix_step)
    loads[3].wait()
    for b in range(slots // 128):
        dest_all[:, pl.ds(b * 128, 128)] = dest_ref[pl.ds(b, n_dp, stride=slots // 128), :]
    dest = dest_all[...]
    inside = (dest >> 9) == me_g
    rank = dot_nn(inside.astype(F32).astype(BF), prefix[...])
    ranks[...] = jnp.where(inside, rank, -1.0)
    row_of[...] = (dest - me_g * rows).astype(F32)

    def rows_step(s):
        hit = iota((cap, slots), 0).astype(F32) == ranks[pl.ds(s, 1), :]
        row = jnp.sum(jnp.where(hit, row_of[pl.ds(s, 1), :] + 1.0, 0.0), axis=1, keepdims=True)
        chosen = (row == (iota((cap, rows), 1) + 1).astype(F32)).astype(F32)
        pick_wide[pl.ds(s * 32, 32), :] = chosen[:32]
        pick_wide[pl.ds(main + s * 8, 8), :] = chosen[32:]

    for s in range(n_dp):
        rows_step(s)

    def narrow_step(i):
        pick_rows[at(i, 128), :] = pick_wide[at(i, 128), :].astype(BF)

    loop(n_lanes // 128, narrow_step)
    loads[4].wait()
    product(to_ref(cperm), perm1t, plain(cot_ref), total=rows)
    to_lanes(0, pick_rows, lambda c: cperm[pl.ds(c * 128, 128), :])
    pl.semaphore_wait(barrier, n_feat + n_dp - 2)
    start_dp(0)
    start_feat(GATE1)
    start_feat(UP1)

    mine = dest_all[pl.ds(me_g, 1), :]
    target = mine >> 9
    member = iota((n_dp, slots), 0) == target
    rank = dot_nn(member.astype(F32).astype(BF), prefix[...])
    rank = jnp.sum(jnp.where(member, rank, 0.0), axis=0, keepdims=True).astype(I32)
    lane = jnp.where(rank < 32, target * 32 + rank, main + target * 8 + rank - 32)
    lane = jnp.where(mine >= 0, lane, -1)

    def slots_step(i):
        pick_slots[at(i, 128), :] = (iota((128, slots), 0) + i * 128 == lane).astype(F32).astype(BF)

    loop(n_lanes // 128, slots_step)
    loads[5].wait()
    build_left(lg_ref, mats.at[LG])
    loads[6].wait()
    build_left(lu_ref, mats.at[LU])

    feat_all(GATE1).wait_recv()
    product(to_send(GATE2), mats.at[LG], got(GATE1))
    start_feat(GATE2)
    feat_all(UP1).wait_recv()
    product(to_send(UP2), mats.at[LU], got(UP1))
    start_feat(UP2)

    loads[7].wait()
    loads[8].wait()
    build_right(rd_ref, tmp_a)
    square(mats.at[WD], tmp_a.at[:, pl.ds(0, feats)], perm1)
    build_left(ld_ref, mats.at[LD])
    build_left_back(ld_ref, mats.at[LDT])
    build_right_back(rd_ref, tmp_b.at[:, pl.ds(0, feats)])
    square(mats.at[WDT], perm1t, tmp_b)
    build_left_back(lg_ref, mats.at[LGT])
    build_left_back(lu_ref, mats.at[LUT])
    build_right_back(rg_ref, mats.at[WGT])
    build_right_back(ru_ref, mats.at[WUT])

    dp_all(0).wait_recv()
    for c in range(4):
        value = from_lanes(0, pick_slots, c).astype(BF)
        send[CT, pl.ds(c * 8, 8)] = value.reshape(8, slab, slots)
    start_feat(CT)

    feat_all(GATE2).wait_recv()
    feat_all(UP2).wait_recv()

    def activate(i):
        here = at(i, 128)
        gate = recv[GATE2, :, :, here].reshape(feats, 128).astype(F32)
        up = recv[UP2, :, :, here].reshape(feats, 128).astype(F32)
        scale = 0.7978845608028654
        square_ = gate * gate
        t = jnp.tanh(scale * (gate + 0.044715 * (square_ * gate)))
        half = 0.5 * (1.0 + t)
        gelu = gate * half
        act[:, here] = gelu
        inner = scale * (1.0 + 3 * 0.044715 * square_)
        slope[:, here] = up * (half + 0.5 * gate * ((1.0 - t * t) * inner))
        hidden[:, here] = (gelu * up).astype(BF)

    loop(slots // 128, activate)
    product(to_send(DOWN1), mats.at[WD], plain(hidden))
    start_feat(DOWN1)

    feat_all(CT).wait_recv()
    product(to_send(DSG), mats.at[LDT], got(CT))
    start_feat(DSG)

    feat_all(DOWN1).wait_recv()
    product(to_send(DOWN2), mats.at[LD], got(DOWN1))
    start_feat(DOWN2)
    grad_left(5, DOWN1, CT)

    feat_all(DSG).wait_recv()
    for s, w in tiles(slots, 128):
        hidden_grad = dot_nn(mats[WDT], flat(recv, DSG, s, w))
        to_send(GGRAD)(s, w, hidden_grad * slope[:, pl.ds(s, w)])
        to_send(UGRAD)(s, w, hidden_grad * act[:, pl.ds(s, w)])
    start_feat(GGRAD)
    start_feat(UGRAD)


    product(to_ref(tmp_a), perm1, plain(hidden))
    product(to_ref(tmp_b), perm1, got(DSG))
    grad(4, tmp_a, tmp_b)
    feat_all(DOWN2).wait_recv()
    to_lanes(1, pick_slots, lambda c: recv[DOWN2, pl.ds(c * 8, 8)].reshape(128, slots))
    relay(5)
    relay(4)
    start_dp(1)

    feat_all(GGRAD).wait_recv()
    product(to_send(GSG), mats.at[LGT], got(GGRAD))
    start_feat(GSG)
    feat_all(UGRAD).wait_recv()
    product(to_send(USG), mats.at[LUT], got(UGRAD))
    start_feat(USG)
    grad_left(1, GATE1, GGRAD)
    grad_left(3, UP1, UGRAD)

    feat_all(GSG).wait_recv()
    product(to_ref(tmp_b), perm1, got(GSG))
    grad(0, mixed, tmp_b)
    feat_all(USG).wait_recv()
    product(to_ref(tmp_b), perm1, got(USG))
    grad(2, mixed, tmp_b)
    relay(1)
    relay(3)
    relay(0)
    for s, w in tiles(slots, 256):
        value = dot_nn(mats[WGT], flat(recv, GSG, s, w)) + dot_nn(mats[WUT], flat(recv, USG, s, w))
        mgrad_ref[:, pl.ds(s, w)] = value.astype(BF)
    relay(2)

    dp_all(1).wait_recv()
    for c in range(4):
        cperm[pl.ds(c * 128, 128), :] = from_lanes(1, pick_rows, c).astype(BF)
    product(to_ref(out_ref), perm1, plain(cperm), total=rows)

    for n in (5, 4, 1, 3, 0, 2):
        finish_grad(n)
    for n in range(12):
        feat_all(n).wait_send()
    for n in range(2):
        dp_all(n).wait_send()
    for n in range(6):
        near(n, 0).wait_send()
        near(n, 1).wait_send()
        far_all(n).wait_send()


def hand_over(out_ref, mgrad_ref, grads_ref, out_to, mgrad_to, *grads_to):
    out_to[...] = out_ref[...]
    mgrad_to[...] = mgrad_ref[...]
    for n, ref in enumerate(grads_to):
        ref[...] = grads_ref[n].reshape(ref.shape)


def body(earlier, mix_weights, destinations, cotangent, *factors):
    n_feat, n_dp = lax.axis_size("feat"), lax.axis_size("dp")
    feats, slots = earlier.shape[1:]
    rows = cotangent.shape[1]
    slab = feats // n_feat
    cap = slots // n_dp
    grad_shape = (factors[0].shape[0], factors[0].shape[1] // n_dp, factors[0].shape[2])
    vmem = pl.BlockSpec(memory_space=pltpu.VMEM)
    wide = pltpu.VMEM((feats, slots), BF)
    square = pltpu.VMEM((feats, feats), BF)
    packed = (
        jax.ShapeDtypeStruct((feats, rows), BF),
        jax.ShapeDtypeStruct((feats, slots), BF),
    )
    results = pl.pallas_call(
        kernel,
        out_shape=packed + (jax.ShapeDtypeStruct((6, 32, 128), F32),),
        in_specs=[pl.BlockSpec(memory_space=pltpu.SMEM)] + [pl.BlockSpec(memory_space=pl.ANY)] * 9,
        out_specs=(vmem,) * 3,
        scratch_shapes=[
            pltpu.VMEM(earlier.shape, BF),
            pltpu.VMEM((destinations.size // 128, 128), I32),
            pltpu.VMEM((feats, rows), BF),
            pltpu.VMEM((6,) + factors[0].shape, BF),
            pltpu.SemaphoreType.DMA((9,)),
            pltpu.VMEM((12, n_feat, slab, slots), BF),
            pltpu.VMEM((12, n_feat, slab, slots), BF),
            pltpu.VMEM((2, n_dp, 4 * cap, 128), BF),
            pltpu.VMEM((2, n_dp, 4 * cap, 128), BF),
            pltpu.VMEM((6, 18, 32, 128), BF),
            pltpu.VMEM((6, 2, 5, 32, 128), BF),
            pltpu.VMEM((6, 5, 32, 128), BF),
            pltpu.VMEM((6, 5, 32, 128), BF),
            pltpu.VMEM((n_dp, slots), I32),
            pltpu.VMEM((12, feats, feats), BF),
            square, square, square, square,
            wide, wide, wide, wide,
            pltpu.VMEM((feats, slots), F32),
            pltpu.VMEM((feats, slots), F32),
            pltpu.VMEM((n_dp * cap, rows), BF),
            pltpu.VMEM((n_dp * cap, slots), BF),
            pltpu.VMEM((n_dp * cap, rows), F32),
            pltpu.VMEM((slots, slots), BF),
            pltpu.VMEM((n_dp, slots), F32),
            pltpu.VMEM((n_dp, slots), F32),
            pltpu.VMEM((feats, rows), BF),
            pltpu.SemaphoreType.DMA((12,)),
            pltpu.SemaphoreType.DMA((12,)),
            pltpu.SemaphoreType.DMA((2,)),
            pltpu.SemaphoreType.DMA((2,)),
            pltpu.SemaphoreType.DMA((6, 2)),
            pltpu.SemaphoreType.DMA((6, 2)),
            pltpu.SemaphoreType.DMA((6,)),
            pltpu.SemaphoreType.DMA((6,)),
        ],
        compiler_params=pltpu.CompilerParams(
            collective_id=0, has_side_effects=True, vmem_limit_bytes=60 << 20
        ),
    )(mix_weights, earlier, destinations.reshape(-1, 128), cotangent, *factors)
    return pl.pallas_call(
        hand_over,
        out_shape=packed + (jax.ShapeDtypeStruct(grad_shape, F32),) * 6,
        in_specs=[vmem] * 3,
        out_specs=(vmem,) * 8,
    )(*results)


def solution(mesh):
    factor, grad = P("feat", None, None), P("feat", "dp", None)
    return jax.shard_map(
        body,
        mesh=mesh,
        in_specs=(P(None, "feat", "dp"), P(), P(), P("feat", "dp")) + (factor,) * 6,
        out_specs=(P("feat", "dp"), P("feat", "dp")) + (grad,) * 6,
        check_vma=False,
    )
```

```python
import jax
import jax.numpy as jnp
from jax import lax
from jax.experimental import pallas as pl
from jax.experimental.pallas import tpu as pltpu
from jax.sharding import PartitionSpec as P

MESH = pl.DeviceIdType.MESH
BF = jnp.bfloat16
F32 = jnp.float32
I32 = jnp.int32

GATE1, UP1, GATE2, UP2, DOWN1, DOWN2, CT, DSG, GGRAD, UGRAD, GSG, USG = range(12)
WG, WGT, WU, WUT, WD, WDT, LG, LGT, LU, LUT, LD, LDT = range(12)


def dot_nn(a, b):
    return lax.dot_general(a, b, (((1,), (0,)), ((), ())), preferred_element_type=F32)


def dot_nt(a, b):
    return lax.dot_general(a, b, (((1,), (1,)), ((), ())), preferred_element_type=F32)


def dot_tn(a, b):
    return lax.dot_general(a, b, (((0,), (0,)), ((), ())), preferred_element_type=F32)


def tiles(total, width):
    return [(s, min(width, total - s)) for s in range(0, total, width)]


def loop(count, step):
    def run(i, carry):
        step(i)
        return carry

    lax.fori_loop(0, count, run, 0)


def at(i, width):
    return pl.ds(pl.multiple_of(i * width, width), width)


def iota(shape, dim):
    return lax.broadcasted_iota(I32, shape, dim)


def kernel(
    weights_ref, earlier_in, dest_in, cot_in, rg_in, lg_in, ru_in, lu_in, rd_in, ld_in,
    out_ref, mgrad_ref, grads_ref,
    earlier_ref, dest_ref, cot_ref, factors, isem,
    send, recv, zsend, zrecv, gsend, gnear, gsum, gfar, gall, gland, dest_all, mats, perm1t, perm1, perm2t, perm2, tmp_a, tmp_b,
    mixed, hidden, act, slope, pick_rows, pick_slots, pick_wide, prefix, ranks, row_of, cperm,
    ssem, rsem, zssem, zrsem, nssem, nrsem, fssem, frsem, dssem, drsem,
):
    n_feat, slab, slots = send.shape[1:]
    n_dp, lanes_out, width = zsend.shape[1:]
    feats, rows = cot_in.shape
    me_f = lax.axis_index("feat")
    me_g = lax.axis_index("dp")
    cap = lanes_out // 4
    n_lanes = n_dp * cap
    main = n_dp * 32

    def feat_peer(k):
        return lax.rem(me_f + lax.rem(k * 11, n_feat), n_feat)

    def dp_peer(i):
        return lax.rem(me_g + 8 + ((i + 1) // 2) * (1 - 2 * lax.rem(i, 2)), n_dp)

    rg_ref, lg_ref, ru_ref, lu_ref, rd_ref, ld_ref = (factors.at[n] for n in range(6))
    loads = [
        pltpu.make_async_copy(source, target, isem.at[n])
        for n, (source, target) in enumerate((
            (earlier_in, earlier_ref), (rg_in, rg_ref), (ru_in, ru_ref), (dest_in, dest_ref),
            (cot_in, cot_ref), (lg_in, lg_ref), (lu_in, lu_ref), (rd_in, rd_ref), (ld_in, ld_ref),
        ))
    ]
    for load in loads:
        load.start()
    barrier = pltpu.get_barrier_semaphore()
    loop(n_feat - 1, lambda i: pl.semaphore_signal(
        barrier, inc=1, device_id={"feat": feat_peer(i + 1)}, device_id_type=MESH))
    loop(n_dp - 1, lambda i: pl.semaphore_signal(
        barrier, inc=1, device_id={"dp": dp_peer(i)}, device_id_type=MESH))

    def start_feat(n):
        def step(i):
            peer = feat_peer(i + 1)
            pltpu.make_async_remote_copy(
                src_ref=send.at[n, peer], dst_ref=recv.at[n, me_f],
                send_sem=ssem.at[n], recv_sem=rsem.at[n],
                device_id={"feat": peer}, device_id_type=MESH,
            ).start()

        loop(n_feat - 1, step)
        recv[n, me_f] = send[n, me_f]

    def feat_all(n):
        return pltpu.make_async_remote_copy(
            src_ref=send.at[n, pl.ds(0, n_feat - 1)], dst_ref=recv.at[n, pl.ds(0, n_feat - 1)],
            send_sem=ssem.at[n], recv_sem=rsem.at[n],
            device_id={"feat": feat_peer(1)}, device_id_type=MESH,
        )

    def start_dp(n):
        def step(i):
            peer = dp_peer(i)
            pltpu.make_async_remote_copy(
                src_ref=zsend.at[n, peer], dst_ref=zrecv.at[n, me_g],
                send_sem=zssem.at[n], recv_sem=zrsem.at[n],
                device_id={"dp": peer}, device_id_type=MESH,
            ).start()

        loop(n_dp - 1, step)
        zrecv[n, me_g] = zsend[n, me_g]

    def dp_all(n):
        return pltpu.make_async_remote_copy(
            src_ref=zsend.at[n, pl.ds(0, n_dp - 1)], dst_ref=zrecv.at[n, pl.ds(0, n_dp - 1)],
            send_sem=zssem.at[n], recv_sem=zrsem.at[n],
            device_id={"dp": dp_peer(0)}, device_id_type=MESH,
        )

    def near(n, h):
        return pltpu.make_async_remote_copy(
            src_ref=gsend.at[n, pl.ds(12 * h, 5)], dst_ref=gnear.at[n, h],
            send_sem=nssem.at[n, h], recv_sem=nrsem.at[n, h],
            device_id={"dp": lax.rem(me_g + (1, n_dp - 1)[h], n_dp)}, device_id_type=MESH,
        )

    def far(n, j):
        return pltpu.make_async_remote_copy(
            src_ref=gsum.at[n, j], dst_ref=gfar.at[n, j],
            send_sem=fssem.at[n], recv_sem=frsem.at[n],
            device_id={"dp": lax.rem(me_g + 2 * n_dp - 2 - 3 * j, n_dp)}, device_id_type=MESH,
        )

    def far_all(n):
        return pltpu.make_async_remote_copy(
            src_ref=gsum.at[n], dst_ref=gfar.at[n], send_sem=fssem.at[n], recv_sem=frsem.at[n],
            device_id={"dp": lax.rem(me_g + 1, n_dp)}, device_id_type=MESH,
        )

    def relay(n):
        near(n, 0).wait_recv()
        near(n, 1).wait_recv()
        total = gsend[n, pl.ds(6, 5)].astype(F32) + gnear[n, 0].astype(F32) + gnear[n, 1].astype(F32)
        gsum[n] = total.astype(BF)
        for j in range(5):
            far(n, j).start()

    def build_perms():
        def step(i):
            here = at(i, 128)
            r, c = iota((128, feats), 0) + i * 128, iota((128, feats), 1)
            q, a, b = r >> 4, (r >> 2) & 3, r & 3
            perm1t[here, :] = (c == a * 128 + 4 * q + b).astype(F32).astype(BF)
            perm2t[here, :] = (c == b * 128 + 4 * q + a).astype(F32).astype(BF)
            q, a, b = c >> 4, (c >> 2) & 3, c & 3
            perm1[here, :] = (r == a * 128 + 4 * q + b).astype(F32).astype(BF)
            perm2[here, :] = (r == b * 128 + 4 * q + a).astype(F32).astype(BF)

        loop(feats // 128, step)

    def square(dst, first, second):
        for s, w in tiles(feats, 256):
            dst[:, pl.ds(s, w)] = dot_nn(first[...], second[:, pl.ds(s, w)]).astype(BF)

    def build_right(factor, w):
        def step(i):
            w[:, at(i, 128)] = dot_nt(perm1t[:, at(i, 128)], factor[i]).astype(BF)

        loop(4, step)

    def build_right_back(factor, wt):
        def step(i):
            wt[at(i, 128), :] = dot_nt(factor[i], perm1t[:, at(i, 128)]).astype(BF)

        loop(4, step)

    def build_left(factor, w):
        def step(i):
            tmp_b[:, at(i, 128)] = dot_nt(perm2t[:, at(i, 128)], factor[i]).astype(BF)

        loop(4, step)
        square(w, tmp_b.at[:, pl.ds(0, feats)], perm2)

    def build_left_back(factor, wt):
        def step(i):
            tmp_a[:, at(i, 128)] = dot_nn(perm2t[:, at(i, 128)], factor[i]).astype(BF)

        loop(4, step)
        square(wt, tmp_a.at[:, pl.ds(0, feats)], perm2)

    def flat(ref, n, s, w):
        return ref[n, :, :, pl.ds(s, w)].reshape(feats, w)

    def got(n):
        return lambda s, w: flat(recv, n, s, w)

    def plain(ref):
        return lambda s, w: ref[:, pl.ds(s, w)]

    def to_send(n):
        def put(s, w, value):
            send[n, :, :, pl.ds(s, w)] = value.astype(BF).reshape(n_feat, slab, w)

        return put

    def to_ref(ref):
        def put(s, w, value):
            ref[:, pl.ds(s, w)] = value.astype(ref.dtype)

        return put

    def product(put, mat, load, total=slots, step=256):
        for s, w in tiles(total, step):
            put(s, w, dot_nn(mat[...], load(s, w)))

    def to_lanes(n, pick, load):
        rest = []
        for c in range(4):
            value = dot_nt(pick[...], load(c))
            zsend[n, :, pl.ds(c * 32, 32), :] = value[:main].reshape(n_dp, 32, width).astype(BF)
            rest.append(value[main:].reshape(n_dp, 8, width))
        for h in range(2):
            pair = jnp.concatenate(rest[2 * h : 2 * h + 2], axis=1).astype(BF)
            zsend[n, :, pl.ds(128 + 16 * h, 16), :] = pair

    def from_lanes(n, pick, c):
        head = zrecv[n, :, pl.ds(c * 32, 32), :].reshape(main, width)
        pair = zrecv[n, :, pl.ds(128 + 16 * (c // 2), 16), :].astype(F32)
        tail = pair[:, 8 * (c % 2) : 8 * (c % 2) + 8, :].reshape(n_dp * 8, width).astype(BF)
        return dot_tn(jnp.concatenate([head, tail], axis=0), pick[...])

    def shares(first, second):
        parts = []
        for c in range(4):
            here = pl.ds(c * 128, 128)
            parts.append(dot_nt(first[here, :], second[here, :]).reshape(n_dp, 8, 128))
        return jnp.concatenate(parts, axis=1).astype(BF)

    def grad(n, first, second):
        packed = shares(first, second)
        for g in range(n_dp):
            m = lax.rem(me_g + 2 * n_dp - 1 - g, n_dp)
            gsend[n, lax.rem(m, 3) * 6 + m // 3] = packed[g]
        near(n, 0).start()
        near(n, 1).start()

    def grad_left(n, spread, outgrad):
        product(to_ref(tmp_a), perm2, got(spread))
        product(to_ref(tmp_b), perm2, got(outgrad))
        grad(n, tmp_a, tmp_b)

    def grad_direct(first, second):
        gall[...] = shares(first, second)

        def step(i):
            peer = dp_peer(i)
            pltpu.make_async_remote_copy(
                src_ref=gall.at[peer], dst_ref=gland.at[me_g], send_sem=dssem, recv_sem=drsem,
                device_id={"dp": peer}, device_id_type=MESH,
            ).start()

        loop(n_dp - 1, step)
        gland[me_g] = gall[me_g]

    def direct_all():
        return pltpu.make_async_remote_copy(
            src_ref=gall.at[pl.ds(0, n_dp - 1)], dst_ref=gland.at[pl.ds(0, n_dp - 1)],
            send_sem=dssem, recv_sem=drsem,
            device_id={"dp": dp_peer(0)}, device_id_type=MESH,
        )

    def finish_grad(n):
        far_all(n).wait_recv()
        total = gsend[n, 5].astype(F32) + jnp.sum(gfar[n].astype(F32), axis=0)
        grads_ref[n] = total * ((rows * n_dp) ** (-0.5))

    def mix(i):
        here = at(i, 64)
        total = jnp.zeros((64, slots), F32)
        for k in range(earlier_ref.shape[0]):
            total = total + weights_ref[k] * earlier_ref[k, here, :].astype(F32)
        mixed[here, :] = total.astype(BF)

    build_perms()
    loads[0].wait()
    loop(feats // 64, mix)
    loads[1].wait()
    build_right(rg_ref, mats.at[WG])
    product(to_send(GATE1), mats.at[WG], plain(mixed))
    loads[2].wait()
    build_right(ru_ref, mats.at[WU])
    product(to_send(UP1), mats.at[WU], plain(mixed))

    def prefix_step(i):
        r, c = iota((128, slots), 0) + i * 128, iota((128, slots), 1)
        prefix[at(i, 128), :] = (r < c).astype(F32).astype(BF)

    loop(slots // 128, prefix_step)
    loads[3].wait()
    for b in range(slots // 128):
        dest_all[:, pl.ds(b * 128, 128)] = dest_ref[pl.ds(b, n_dp, stride=slots // 128), :]
    dest = dest_all[...]
    inside = (dest >> 9) == me_g
    rank = dot_nn(inside.astype(F32).astype(BF), prefix[...])
    ranks[...] = jnp.where(inside, rank, -1.0)
    row_of[...] = (dest - me_g * rows).astype(F32)

    def rows_step(s):
        hit = iota((cap, slots), 0).astype(F32) == ranks[pl.ds(s, 1), :]
        row = jnp.sum(jnp.where(hit, row_of[pl.ds(s, 1), :] + 1.0, 0.0), axis=1, keepdims=True)
        chosen = (row == (iota((cap, rows), 1) + 1).astype(F32)).astype(F32)
        pick_wide[pl.ds(s * 32, 32), :] = chosen[:32]
        pick_wide[pl.ds(main + s * 8, 8), :] = chosen[32:]

    for s in range(n_dp):
        rows_step(s)

    def narrow_step(i):
        pick_rows[at(i, 128), :] = pick_wide[at(i, 128), :].astype(BF)

    loop(n_lanes // 128, narrow_step)
    loads[4].wait()
    product(to_ref(cperm), perm1t, plain(cot_ref), total=rows)
    to_lanes(0, pick_rows, lambda c: cperm[pl.ds(c * 128, 128), :])
    pl.semaphore_wait(barrier, n_feat + n_dp - 2)
    start_dp(0)
    start_feat(GATE1)
    start_feat(UP1)

    mine = dest_all[pl.ds(me_g, 1), :]
    target = mine >> 9
    member = iota((n_dp, slots), 0) == target
    rank = dot_nn(member.astype(F32).astype(BF), prefix[...])
    rank = jnp.sum(jnp.where(member, rank, 0.0), axis=0, keepdims=True).astype(I32)
    lane = jnp.where(rank < 32, target * 32 + rank, main + target * 8 + rank - 32)
    lane = jnp.where(mine >= 0, lane, -1)

    def slots_step(i):
        pick_slots[at(i, 128), :] = (iota((128, slots), 0) + i * 128 == lane).astype(F32).astype(BF)

    loop(n_lanes // 128, slots_step)
    loads[5].wait()
    build_left(lg_ref, mats.at[LG])
    loads[6].wait()
    build_left(lu_ref, mats.at[LU])

    feat_all(GATE1).wait_recv()
    product(to_send(GATE2), mats.at[LG], got(GATE1))
    start_feat(GATE2)
    feat_all(UP1).wait_recv()
    product(to_send(UP2), mats.at[LU], got(UP1))
    start_feat(UP2)

    loads[7].wait()
    loads[8].wait()
    build_right(rd_ref, tmp_a)
    square(mats.at[WD], tmp_a.at[:, pl.ds(0, feats)], perm1)
    build_left(ld_ref, mats.at[LD])
    build_left_back(ld_ref, mats.at[LDT])
    build_right_back(rd_ref, tmp_b.at[:, pl.ds(0, feats)])
    square(mats.at[WDT], perm1t, tmp_b)
    build_left_back(lg_ref, mats.at[LGT])
    build_left_back(lu_ref, mats.at[LUT])
    build_right_back(rg_ref, mats.at[WGT])
    build_right_back(ru_ref, mats.at[WUT])

    dp_all(0).wait_recv()
    for c in range(4):
        value = from_lanes(0, pick_slots, c).astype(BF)
        send[CT, pl.ds(c * 8, 8)] = value.reshape(8, slab, slots)
    start_feat(CT)

    feat_all(GATE2).wait_recv()
    feat_all(UP2).wait_recv()

    def activate(i):
        here = at(i, 128)
        gate = recv[GATE2, :, :, here].reshape(feats, 128).astype(F32)
        up = recv[UP2, :, :, here].reshape(feats, 128).astype(F32)
        scale = 0.7978845608028654
        square_ = gate * gate
        t = jnp.tanh(scale * (gate + 0.044715 * (square_ * gate)))
        half = 0.5 * (1.0 + t)
        gelu = gate * half
        act[:, here] = gelu
        inner = scale * (1.0 + 3 * 0.044715 * square_)
        slope[:, here] = up * (half + 0.5 * gate * ((1.0 - t * t) * inner))
        hidden[:, here] = (gelu * up).astype(BF)

    loop(slots // 128, activate)
    product(to_send(DOWN1), mats.at[WD], plain(hidden))
    start_feat(DOWN1)

    feat_all(DOWN1).wait_recv()
    product(to_send(DOWN2), mats.at[LD], got(DOWN1))
    start_feat(DOWN2)
    feat_all(CT).wait_recv()
    product(to_send(DSG), mats.at[LDT], got(CT))
    start_feat(DSG)
    grad_left(5, DOWN1, CT)
    feat_all(DOWN2).wait_recv()
    to_lanes(1, pick_slots, lambda c: recv[DOWN2, pl.ds(c * 8, 8)].reshape(128, slots))
    relay(5)
    start_dp(1)

    feat_all(DSG).wait_recv()
    for s, w in tiles(slots, 128):
        hidden_grad = dot_nn(mats[WDT], flat(recv, DSG, s, w))
        to_send(GGRAD)(s, w, hidden_grad * slope[:, pl.ds(s, w)])
        to_send(UGRAD)(s, w, hidden_grad * act[:, pl.ds(s, w)])
    start_feat(GGRAD)
    start_feat(UGRAD)


    product(to_ref(tmp_a), perm1, plain(hidden))
    product(to_ref(tmp_b), perm1, got(DSG))
    grad(4, tmp_a, tmp_b)

    feat_all(GGRAD).wait_recv()
    product(to_send(GSG), mats.at[LGT], got(GGRAD))
    start_feat(GSG)
    feat_all(UGRAD).wait_recv()
    product(to_send(USG), mats.at[LUT], got(UGRAD))
    start_feat(USG)
    grad_left(1, GATE1, GGRAD)
    grad_left(3, UP1, UGRAD)

    feat_all(GSG).wait_recv()
    product(to_ref(tmp_b), perm1, got(GSG))
    grad(0, mixed, tmp_b)
    relay(4)
    relay(1)
    relay(3)
    feat_all(USG).wait_recv()
    product(to_ref(tmp_b), perm1, got(USG))
    grad_direct(mixed, tmp_b)
    relay(0)
    for s, w in tiles(slots, 256):
        value = dot_nn(mats[WGT], flat(recv, GSG, s, w)) + dot_nn(mats[WUT], flat(recv, USG, s, w))
        mgrad_ref[:, pl.ds(s, w)] = value.astype(BF)
    dp_all(1).wait_recv()
    for c in range(4):
        cperm[pl.ds(c * 128, 128), :] = from_lanes(1, pick_rows, c).astype(BF)
    product(to_ref(out_ref), perm1, plain(cperm), total=rows)

    for n in (5, 4, 1, 3, 0):
        finish_grad(n)
    direct_all().wait_recv()
    grads_ref[2] = jnp.sum(gland[...].astype(F32), axis=0) * ((rows * n_dp) ** (-0.5))
    for n in range(12):
        feat_all(n).wait_send()
    for n in range(2):
        dp_all(n).wait_send()
    direct_all().wait_send()
    for n in (0, 1, 3, 4, 5):
        near(n, 0).wait_send()
        near(n, 1).wait_send()
        far_all(n).wait_send()


def hand_over(out_ref, mgrad_ref, grads_ref, out_to, mgrad_to, *grads_to):
    out_to[...] = out_ref[...]
    mgrad_to[...] = mgrad_ref[...]
    for n, ref in enumerate(grads_to):
        ref[...] = grads_ref[n].reshape(ref.shape)


def body(earlier, mix_weights, destinations, cotangent, *factors):
    n_feat, n_dp = lax.axis_size("feat"), lax.axis_size("dp")
    feats, slots = earlier.shape[1:]
    rows = cotangent.shape[1]
    slab = feats // n_feat
    cap = slots // n_dp
    grad_shape = (factors[0].shape[0], factors[0].shape[1] // n_dp, factors[0].shape[2])
    vmem = pl.BlockSpec(memory_space=pltpu.VMEM)
    wide = pltpu.VMEM((feats, slots), BF)
    square = pltpu.VMEM((feats, feats), BF)
    packed = (
        jax.ShapeDtypeStruct((feats, rows), BF),
        jax.ShapeDtypeStruct((feats, slots), BF),
    )
    results = pl.pallas_call(
        kernel,
        out_shape=packed + (jax.ShapeDtypeStruct((6, 32, 128), F32),),
        in_specs=[pl.BlockSpec(memory_space=pltpu.SMEM)] + [pl.BlockSpec(memory_space=pl.ANY)] * 9,
        out_specs=(vmem,) * 3,
        scratch_shapes=[
            pltpu.VMEM(earlier.shape, BF),
            pltpu.VMEM((destinations.size // 128, 128), I32),
            pltpu.VMEM((feats, rows), BF),
            pltpu.VMEM((6,) + factors[0].shape, BF),
            pltpu.SemaphoreType.DMA((9,)),
            pltpu.VMEM((12, n_feat, slab, slots), BF),
            pltpu.VMEM((12, n_feat, slab, slots), BF),
            pltpu.VMEM((2, n_dp, 4 * cap, 128), BF),
            pltpu.VMEM((2, n_dp, 4 * cap, 128), BF),
            pltpu.VMEM((6, 18, 32, 128), BF),
            pltpu.VMEM((6, 2, 5, 32, 128), BF),
            pltpu.VMEM((6, 5, 32, 128), BF),
            pltpu.VMEM((6, 5, 32, 128), BF),
            pltpu.VMEM((n_dp, 32, 128), BF),
            pltpu.VMEM((n_dp, 32, 128), BF),
            pltpu.VMEM((n_dp, slots), I32),
            pltpu.VMEM((12, feats, feats), BF),
            square, square, square, square,
            wide, wide, wide, wide,
            pltpu.VMEM((feats, slots), F32),
            pltpu.VMEM((feats, slots), F32),
            pltpu.VMEM((n_dp * cap, rows), BF),
            pltpu.VMEM((n_dp * cap, slots), BF),
            pltpu.VMEM((n_dp * cap, rows), F32),
            pltpu.VMEM((slots, slots), BF),
            pltpu.VMEM((n_dp, slots), F32),
            pltpu.VMEM((n_dp, slots), F32),
            pltpu.VMEM((feats, rows), BF),
            pltpu.SemaphoreType.DMA((12,)),
            pltpu.SemaphoreType.DMA((12,)),
            pltpu.SemaphoreType.DMA((2,)),
            pltpu.SemaphoreType.DMA((2,)),
            pltpu.SemaphoreType.DMA((6, 2)),
            pltpu.SemaphoreType.DMA((6, 2)),
            pltpu.SemaphoreType.DMA((6,)),
            pltpu.SemaphoreType.DMA((6,)),
            pltpu.SemaphoreType.DMA,
            pltpu.SemaphoreType.DMA,
        ],
        compiler_params=pltpu.CompilerParams(
            collective_id=0, has_side_effects=True, vmem_limit_bytes=60 << 20
        ),
    )(mix_weights, earlier, destinations.reshape(-1, 128), cotangent, *factors)
    return pl.pallas_call(
        hand_over,
        out_shape=packed + (jax.ShapeDtypeStruct(grad_shape, F32),) * 6,
        in_specs=[vmem] * 3,
        out_specs=(vmem,) * 8,
    )(*results)


def solution(mesh):
    factor, grad = P("feat", None, None), P("feat", "dp", None)
    return jax.shard_map(
        body,
        mesh=mesh,
        in_specs=(P(None, "feat", "dp"), P(), P(), P("feat", "dp")) + (factor,) * 6,
        out_specs=(P("feat", "dp"), P("feat", "dp")) + (grad,) * 6,
        check_vma=False,
    )
```
